32 devices in a mesh: groups: 2 (over x), seq: 16 (over z, y, core).
Axes of the slice: x: 2, y: 2, z: 4, core: 2. Of those that a mesh axis runs over, the one named last changes fastest.
Arguments:
- signal: bfloat16 [32768, 768], P(('groups', 'seq')), parts along dimension 0, may hold values from -6 to 6
- norm_gain: float32 [768], replicated, may hold values from 0.1 to 1.9
- conv_weight: bfloat16 [3, 768, 384], replicated, may hold values from -0.125 to 0.125
- output_weight: bfloat16 [384, 768], replicated, may hold values from -0.3125 to 0.3125
- cotangent: bfloat16 [32768, 768], P(('groups', 'seq')), parts along dimension 0, may hold values from -6 to 6
Outputs:
- block_out: bfloat16 [32768, 768], P(('groups', 'seq')), parts along dimension 0
- signal_grad: bfloat16 [32768, 768], P(('groups', 'seq')), parts along dimension 0
- conv_grad: float32 [6, 768, 384], P('groups'), parts along dimension 0
- output_grad: float32 [768, 768], P('groups'), parts along dimension 0
The draws below stay inside these ranges and needn't reach their ends.
There are 2 independent parts, one for each index of `groups`. The reference program is written for one: setup_inputs(seed, part) draws one part's arguments, and reference() takes and returns one part's arrays. A program takes and returns all parts, laid end to end along the dimension named above; an argument that names none is the same for every part. Nothing has to cross between parts.
All inputs are finite; a program needn't handle non-finite values.
Results may differ from the reference program's by a relative error of at most 0.0056.
Values may be sent and summed in bfloat16 or wider, within the bound.
A program may use at most 128 MiB of HBM per device.

```python
import math
import jax
import jax.numpy as jnp
from jax import lax

STREAM_CHANNELS = 768
H = 384
BINS = 16384


def raised(entries, rng, source, target, parts, factor):
    owner, partner = [(jnp.arange(entries.shape[axis_at]) // (entries.shape[axis_at] // parts)).reshape([-1 if axis == axis_at else 1 for axis in range(entries.ndim)]) for axis_at in (source, target)]
    chosen = jax.random.permutation(rng, parts)[partner]
    strong = (owner == chosen) | (owner == (partner + parts // 2) % parts)
    return jnp.where(strong, factor * entries, entries)


def shard_levels(key, extent, cuts, smallest, top_value):
    def one(position, parts):
        draws = jax.random.uniform(jax.random.fold_in(jax.random.fold_in(key, 6), position), (parts,), jnp.float32, smallest / len(cuts), top_value / len(cuts))
        return jnp.repeat(jnp.exp(draws), extent[position] // parts).reshape((-1,) + (1,) * (len(extent) - position - 1))

    loudness = one(*cuts[0])
    for cut in cuts[1:]:
        loudness = loudness * one(*cut)
    return loudness


def noise(rng, extent, scale, bound, pieces=(), kind=jnp.bfloat16):
    result = jax.random.normal(rng, extent, jnp.float32) * scale
    if len(pieces) > 0:
        result = shard_levels(rng, extent, pieces, -0.22, 0.18) * result
    return jnp.clip(result, min=-bound, max=bound).astype(kind)


def gaussian_with(rng, extent, width, reach, pieces, heavy, held_as=jnp.bfloat16):
    result = width * jax.random.normal(rng, extent, jnp.float32)
    if pieces:
        result = result * shard_levels(rng, extent, pieces, -0.22, 0.18)
    return jnp.clip(raised(result, jax.random.fold_in(rng, 3), *heavy), -reach, reach).astype(held_as)


def setup_inputs(seed: int = 0, part: int = 0) -> dict:
    arg_keys = jax.random.split(jax.random.key(seed), 6)
    part_keys = jax.random.split(jax.random.fold_in(arg_keys[5], part), 6)
    signal = gaussian_with(part_keys[0], (BINS, STREAM_CHANNELS), 1.0, 6.0, ((0, 16),), (0, 1, 16, 2.0))
    norm_gain = jnp.clip(1.0 + 0.18 * jax.random.normal(arg_keys[1], (STREAM_CHANNELS,), jnp.float32), 0.1, 1.9)
    conv_weight = noise(arg_keys[2], (3, STREAM_CHANNELS, H), (3 * STREAM_CHANNELS) ** -0.5, 0.125)
    output_weight = noise(arg_keys[3], (H, STREAM_CHANNELS), H ** -0.5, 0.3125)
    cotangent = gaussian_with(part_keys[4], (BINS, STREAM_CHANNELS), 1.0, 6.0, ((0, 16),), (0, 1, 16, 2.0))
    return {"signal": signal, "norm_gain": norm_gain, "conv_weight": conv_weight, "output_weight": output_weight, "cotangent": cotangent}


epsilon = 1e-06

def gelu_slope(value):
    return 0.5 * (1.0 + jax.scipy.special.erf(value * (1.0 / math.sqrt(2.0)))) + value * jnp.exp(-0.5 * value * value) * (1.0 / math.sqrt(2.0 * math.pi))

def reference(signal, norm_gain, conv_weight, output_weight, cotangent):
    dilation = BINS // 8
    signal_f = signal.astype(jnp.float32)
    mean_square = lax.optimization_barrier(jnp.mean(signal_f * signal_f, axis=-1, keepdims=True))
    inverse_rms = lax.rsqrt(mean_square + epsilon)
    normed = signal_f * inverse_rms * norm_gain
    activated_signal = jax.nn.gelu(normed, approximate=False).astype(jnp.bfloat16)
    empty_rows = jnp.zeros((dilation, STREAM_CHANNELS), jnp.bfloat16)
    earlier_taps = jnp.concatenate([empty_rows, activated_signal[:-dilation]], axis=0)
    later_taps = jnp.concatenate([activated_signal[dilation:], empty_rows], axis=0)
    hidden = jnp.dot(earlier_taps, conv_weight[0], preferred_element_type=jnp.float32)
    hidden = hidden + jnp.dot(activated_signal, conv_weight[1], preferred_element_type=jnp.float32)
    hidden = hidden + jnp.dot(later_taps, conv_weight[2], preferred_element_type=jnp.float32)
    gated = jax.nn.gelu(hidden, approximate=False).astype(jnp.bfloat16)
    block_out = (signal_f + jnp.dot(gated, output_weight, preferred_element_type=jnp.float32)).astype(jnp.bfloat16)
    grad_scale = 1.0 / math.sqrt(BINS)
    gated_grad = jnp.dot(cotangent, output_weight.T, preferred_element_type=jnp.float32)
    hidden_grad = (gated_grad * gelu_slope(hidden)).astype(jnp.bfloat16)
    output_grad = jnp.dot(gated.T, cotangent, preferred_element_type=jnp.float32) * grad_scale
    conv_grad = jnp.stack([jnp.dot(earlier_taps.T, hidden_grad, preferred_element_type=jnp.float32), jnp.dot(activated_signal.T, hidden_grad, preferred_element_type=jnp.float32), jnp.dot(later_taps.T, hidden_grad, preferred_element_type=jnp.float32)]) * grad_scale
    leading_tap = jnp.dot(hidden_grad, conv_weight[0].T, preferred_element_type=jnp.float32)
    trailing_tap = jnp.dot(hidden_grad, conv_weight[2].T, preferred_element_type=jnp.float32)
    float_zero_value = jnp.zeros((dilation, STREAM_CHANNELS), jnp.float32)
    input_gradient = jnp.dot(hidden_grad, conv_weight[1].T, preferred_element_type=jnp.float32)
    input_gradient = input_gradient + jnp.concatenate([leading_tap[dilation:], float_zero_value], axis=0)
    input_gradient = input_gradient + jnp.concatenate([float_zero_value, trailing_tap[:-dilation]], axis=0)
    weighted = input_gradient * gelu_slope(normed) * norm_gain
    inner = lax.optimization_barrier(jnp.mean(weighted * signal_f, axis=-1, keepdims=True))
    cubed = inverse_rms * inverse_rms * inverse_rms
    signal_grad = cotangent.astype(jnp.float32) + weighted * inverse_rms - signal_f * cubed * inner
    return (block_out, signal_grad.astype(jnp.bfloat16), conv_grad, output_grad)
```

```python
import math

import jax
import jax.numpy as jnp
from jax import lax
from jax.sharding import PartitionSpec as P

epsilon = 1e-06


def passed_along(block, axis, distance):
    devices = range(lax.axis_size(axis))
    route = [(i - distance, i) for i in devices if i - distance in devices]
    return lax.ppermute(block, axis, route)


def gelu_cdf(value):
    return 0.5 * (1.0 + jax.scipy.special.erf(value * (1.0 / math.sqrt(2.0))))


def gelu_slope(value, cdf):
    return cdf + value * jnp.exp(-0.5 * value * value) * (1.0 / math.sqrt(2.0 * math.pi))


def dot(left, right, contract):
    return lax.dot_general(left, right, (contract, ((), ())), preferred_element_type=jnp.float32)


def shards(signal, norm_gain, conv_weight, output_weight, cotangent):
    devices = lax.axis_size("seq")
    stride = devices // 8
    local_bins = signal.shape[0]
    odd = (lax.axis_index("seq") // stride) % 2 == 1
    far_weight = jnp.where(odd, conv_weight[0], conv_weight[2])
    near_weight = jnp.where(odd, conv_weight[2], conv_weight[0])
    far_route, near_route = [], []
    for i in range(devices):
        is_odd = (i // stride) % 2 == 1
        target = i + 2 * stride if is_odd else i - 2 * stride
        if 0 <= target < devices:
            far_route.append((i, target))
        near_route.append((i, i - stride if is_odd else i + stride))

    signal_f = signal.astype(jnp.float32)
    mean_square = jnp.mean(signal_f * signal_f, axis=-1, keepdims=True)
    inverse_rms = lax.rsqrt(mean_square + epsilon)
    normed = signal_f * inverse_rms * norm_gain
    normed_cdf = gelu_cdf(normed)
    activated = (normed * normed_cdf).astype(jnp.bfloat16)

    chunks = 2
    rows = local_bins // chunks
    parts = []
    for j in range(chunks):
        block = activated[j * rows : (j + 1) * rows]
        far = dot(block, far_weight, ((1,), (0,))).astype(jnp.bfloat16)
        parts.append(lax.ppermute(far, "seq", far_route))
    arrived = []
    for j in range(chunks):
        block = activated[j * rows : (j + 1) * rows]
        near = dot(block, near_weight, ((1,), (0,))) + parts[j].astype(jnp.float32)
        arrived.append(lax.ppermute(near.astype(jnp.bfloat16), "seq", near_route))
    hidden = dot(activated, conv_weight[1], ((1,), (0,))) + jnp.concatenate(arrived).astype(
        jnp.float32
    )
    hidden_cdf = gelu_cdf(hidden)
    gated = (hidden * hidden_cdf).astype(jnp.bfloat16)
    gated_grad = dot(cotangent, output_weight, ((1,), (1,)))
    hidden_grad = (gated_grad * gelu_slope(hidden, hidden_cdf)).astype(jnp.bfloat16)
    earlier = passed_along(hidden_grad, "seq", stride)
    later = passed_along(hidden_grad, "seq", -stride)

    grad_scale = 1.0 / math.sqrt(local_bins * devices)
    block_out = (signal_f + dot(gated, output_weight, ((1,), (0,)))).astype(jnp.bfloat16)
    output_term = dot(gated, cotangent, ((0,), (0,))) * grad_scale
    middle_term = dot(activated, hidden_grad, ((0,), (0,))) * grad_scale
    output_grad, middle_grad = lax.psum((output_term, middle_term), "seq")
    first_term = dot(activated, later, ((0,), (0,))) * grad_scale
    last_term = dot(activated, earlier, ((0,), (0,))) * grad_scale
    first_grad, last_grad = lax.psum((first_term, last_term), "seq")
    conv_grad = jnp.stack([first_grad, middle_grad, last_grad])

    input_gradient = (
        dot(hidden_grad, conv_weight[1], ((1,), (1,)))
        + dot(later, conv_weight[0], ((1,), (1,)))
        + dot(earlier, conv_weight[2], ((1,), (1,)))
    )
    weighted = input_gradient * gelu_slope(normed, normed_cdf) * norm_gain
    inner = jnp.mean(weighted * signal_f, axis=-1, keepdims=True)
    cubed = inverse_rms * inverse_rms * inverse_rms
    signal_grad = cotangent.astype(jnp.float32) + weighted * inverse_rms - signal_f * cubed * inner
    return (block_out, signal_grad.astype(jnp.bfloat16), conv_grad, output_grad)


def solution(mesh):
    placed = (P(("groups", "seq"), None), P(), P(), P(), P(("groups", "seq"), None))
    return jax.shard_map(
        shards,
        mesh=mesh,
        in_specs=placed,
        out_specs=(
            P(("groups", "seq"), None),
            P(("groups", "seq"), None),
            P("groups", None, None),
            P("groups", None),
        ),
        check_vma=False,
    )
```

```python
import functools
import math

import jax
import jax.numpy as jnp
from jax import lax
from jax.experimental import pallas as pl
from jax.experimental.pallas import tpu as pltpu
from jax.sharding import PartitionSpec as P

epsilon = 1e-06


def passed_along(block, axis, distance):
    devices = range(lax.axis_size(axis))
    route = [(i - distance, i) for i in devices if i - distance in devices]
    return lax.ppermute(block, axis, route)


def gelu_cdf(value):
    return 0.5 * (1.0 + jax.scipy.special.erf(value * (1.0 / math.sqrt(2.0))))


def gelu_slope(value, cdf):
    return cdf + value * jnp.exp(-0.5 * value * value) * (1.0 / math.sqrt(2.0 * math.pi))


def dot(left, right, contract):
    return lax.dot_general(left, right, (contract, ((), ())), preferred_element_type=jnp.float32)


def backward(
    devices, signal, cotangent, activated, hidden_grad, gated, conv_weight, norm_gain,
    signal_grad, grads,
    earlier, later, mine, from_sibling, half, pieces,
    halo_send, halo_recv, pair_send, pair_recv, scatter_send, scatter_recv,
    gather_send, gather_recv, back_send, back_recv,
):
    stride = devices // 8
    chips = devices // 2
    channels, width = conv_weight.shape[1:]
    bins = signal.shape[0]
    piece = channels // chips
    me = lax.axis_index("seq")
    chip, core = me // 2, me % 2
    sibling = chip * 2 + 1 - core

    def peer(distance):
        other = lax.rem(chip + distance, chips)
        return other, {"seq": other * 2 + core}

    barrier = pltpu.get_barrier_semaphore()
    pl.semaphore_signal(barrier, inc=1, device_id={"seq": sibling})
    for distance in range(1, chips):
        pl.semaphore_signal(barrier, inc=1, device_id=peer(distance)[1])
    pl.semaphore_wait(barrier, chips)

    has_after, has_before = me + stride < devices, me >= stride
    to_after = pltpu.make_async_remote_copy(
        hidden_grad, earlier, halo_send.at[0], halo_recv.at[0],
        device_id={"seq": lax.rem(me + stride, devices)},
    )
    to_before = pltpu.make_async_remote_copy(
        hidden_grad, later, halo_send.at[1], halo_recv.at[1],
        device_id={"seq": lax.rem(me + devices - stride, devices)},
    )
    pl.when(has_after)(to_after.start)
    pl.when(has_before)(to_before.start)

    @pl.when(jnp.logical_not(has_before))
    def _():
        earlier[...] = jnp.zeros_like(earlier)

    @pl.when(jnp.logical_not(has_after))
    def _():
        later[...] = jnp.zeros_like(later)

    tile = 256

    def contribution(part, left, right):
        @pl.loop(0, channels // tile)
        def _(step):
            at = pl.ds(pl.multiple_of(step * tile, tile), tile)
            mine[part, at, :] = dot(left[:, at], right[...], ((0,), (0,))).astype(jnp.bfloat16)

    def start_pair(batch):
        copy = pltpu.make_async_remote_copy(
            mine.at[2 * batch + 1 - core], from_sibling.at[batch],
            pair_send.at[batch], pair_recv.at[batch], device_id={"seq": sibling},
        )
        copy.start()
        return copy

    def start_scatter(batch):
        half[batch] = (
            mine[2 * batch + core].astype(jnp.float32) + from_sibling[batch].astype(jnp.float32)
        ).astype(jnp.bfloat16)
        copies = []
        for distance in range(1, chips):
            other, device = peer(distance)
            copy = pltpu.make_async_remote_copy(
                half.at[batch, pl.ds(pl.multiple_of(other * piece, piece), piece)],
                pieces.at[batch, distance - 1],
                scatter_send.at[batch, distance - 1], scatter_recv.at[batch, distance - 1],
                device_id=device,
            )
            copy.start()
            copies.append(copy)
        return copies

    def start_gather(batch):
        at = pl.ds(pl.multiple_of(chip * piece, piece), piece)
        total = half[batch, at, :].astype(jnp.float32)
        for distance in range(1, chips):
            total = total + pieces[batch, distance - 1].astype(jnp.float32)
        grads[2 * batch + core, at, :] = total.astype(jnp.bfloat16)
        copies = []
        for distance in range(1, chips):
            copy = pltpu.make_async_remote_copy(
                grads.at[2 * batch + core, at], grads.at[2 * batch + core, at],
                gather_send.at[batch, distance - 1], gather_recv.at[batch, distance - 1],
                device_id=peer(distance)[1],
            )
            copy.start()
            copies.append(copy)
        return copies

    def start_back(batch):
        copy = pltpu.make_async_remote_copy(
            grads.at[2 * batch + core], grads.at[2 * batch + core],
            back_send.at[batch], back_recv.at[batch], device_id={"seq": sibling},
        )
        copy.start()
        return copy

    contribution(0, cotangent, gated)
    contribution(1, activated, hidden_grad)
    pair0 = start_pair(0)
    pair0.wait_recv()
    scatter0 = start_scatter(0)

    pl.when(has_after)(to_before.wait_recv)
    pl.when(has_before)(to_after.wait_recv)
    contribution(2, activated, later)
    contribution(3, activated, earlier)
    pair1 = start_pair(1)
    for copy in scatter0:
        copy.wait_recv()
    gather0 = start_gather(0)
    pair1.wait_recv()
    scatter1 = start_scatter(1)

    @pl.loop(0, bins // tile)
    def _(step):
        at = pl.ds(pl.multiple_of(step * tile, tile), tile)
        signal_f = signal[at, :].astype(jnp.float32)
        mean_square = jnp.mean(signal_f * signal_f, axis=-1, keepdims=True)
        inverse_rms = lax.rsqrt(mean_square + epsilon)
        normed = signal_f * inverse_rms * norm_gain[...]
        input_gradient = (
            dot(hidden_grad[at, :], conv_weight[1], ((1,), (1,)))
            + dot(later[at, :], conv_weight[0], ((1,), (1,)))
            + dot(earlier[at, :], conv_weight[2], ((1,), (1,)))
        )
        weighted = input_gradient * gelu_slope(normed, gelu_cdf(normed)) * norm_gain[...]
        inner = jnp.mean(weighted * signal_f, axis=-1, keepdims=True)
        cubed = inverse_rms * inverse_rms * inverse_rms
        signal_grad[at, :] = (
            cotangent[at, :].astype(jnp.float32)
            + weighted * inverse_rms
            - signal_f * cubed * inner
        ).astype(jnp.bfloat16)

    for copy in gather0:
        copy.wait_recv()
    for copy in gather0:
        copy.wait_send()
    back0 = start_back(0)
    for copy in scatter1:
        copy.wait_recv()
    gather1 = start_gather(1)
    for copy in gather1:
        copy.wait_recv()
    for copy in gather1:
        copy.wait_send()
    back1 = start_back(1)
    back0.wait_recv()
    back1.wait_recv()
    for copy in [pair0, pair1, back0, back1] + scatter0 + scatter1:
        copy.wait_send()
    pl.when(has_after)(to_after.wait_send)
    pl.when(has_before)(to_before.wait_send)


def run_backward(signal, cotangent, activated, hidden_grad, gated, conv_weight, norm_gain):
    devices = lax.axis_size("seq")
    chips = devices // 2
    bins, channels = signal.shape
    width = hidden_grad.shape[1]
    bf16 = jnp.bfloat16
    vmem = pl.BlockSpec(memory_space=pltpu.VMEM)
    dma = pltpu.SemaphoreType.DMA
    return pl.pallas_call(
        functools.partial(backward, devices),
        out_shape=(
            jax.ShapeDtypeStruct((bins, channels), bf16),
            jax.ShapeDtypeStruct((4, channels, width), bf16),
        ),
        in_specs=[vmem] * 7,
        out_specs=(vmem, vmem),
        scratch_shapes=[
            pltpu.VMEM((bins, width), bf16),
            pltpu.VMEM((bins, width), bf16),
            pltpu.VMEM((4, channels, width), bf16),
            pltpu.VMEM((2, channels, width), bf16),
            pltpu.VMEM((2, channels, width), bf16),
            pltpu.VMEM((2, chips - 1, channels // chips, width), bf16),
            dma((2,)), dma((2,)), dma((2,)), dma((2,)),
            dma((2, chips - 1)), dma((2, chips - 1)), dma((2, chips - 1)), dma((2, chips - 1)),
            dma((2,)), dma((2,)),
        ],
        compiler_params=pltpu.CompilerParams(
            collective_id=0, has_side_effects=True, vmem_limit_bytes=48 << 20
        ),
        name="backward",
    )(signal, cotangent, activated, hidden_grad, gated, conv_weight, norm_gain.reshape(1, -1))


def shards(signal, norm_gain, conv_weight, output_weight, cotangent):
    devices = lax.axis_size("seq")
    stride = devices // 8
    local_bins = signal.shape[0]
    odd = (lax.axis_index("seq") // stride) % 2 == 1
    far_weight = jnp.where(odd, conv_weight[0], conv_weight[2])
    near_weight = jnp.where(odd, conv_weight[2], conv_weight[0])
    far_route, near_route = [], []
    for i in range(devices):
        is_odd = (i // stride) % 2 == 1
        target = i + 2 * stride if is_odd else i - 2 * stride
        if 0 <= target < devices:
            far_route.append((i, target))
        near_route.append((i, i - stride if is_odd else i + stride))

    signal_f = signal.astype(jnp.float32)
    mean_square = jnp.mean(signal_f * signal_f, axis=-1, keepdims=True)
    inverse_rms = lax.rsqrt(mean_square + epsilon)
    normed = signal_f * inverse_rms * norm_gain
    normed_cdf = gelu_cdf(normed)
    activated = (normed * normed_cdf).astype(jnp.bfloat16)

    chunks = 2
    rows = local_bins // chunks
    parts = []
    for j in range(chunks):
        block = activated[j * rows : (j + 1) * rows]
        far = dot(block, far_weight, ((1,), (0,))).astype(jnp.bfloat16)
        parts.append(lax.ppermute(far, "seq", far_route))
    arrived = []
    for j in range(chunks):
        block = activated[j * rows : (j + 1) * rows]
        near = dot(block, near_weight, ((1,), (0,))) + parts[j].astype(jnp.float32)
        arrived.append(lax.ppermute(near.astype(jnp.bfloat16), "seq", near_route))
    hidden = dot(activated, conv_weight[1], ((1,), (0,))) + jnp.concatenate(arrived).astype(
        jnp.float32
    )
    hidden_cdf = gelu_cdf(hidden)
    gated = (hidden * hidden_cdf).astype(jnp.bfloat16)
    gated_grad = dot(cotangent, output_weight, ((1,), (1,)))
    hidden_grad = (gated_grad * gelu_slope(hidden, hidden_cdf)).astype(jnp.bfloat16)
    if (signal.shape[1] * 2 // devices) % 16 == 0:
        block_out = (signal_f + dot(gated, output_weight, ((1,), (0,)))).astype(jnp.bfloat16)
        signal_grad, grads = run_backward(
            signal, cotangent, activated, hidden_grad, gated, conv_weight, norm_gain
        )
        grads = grads.astype(jnp.float32) * (1.0 / math.sqrt(local_bins * devices))
        conv_grad = jnp.stack([grads[2], grads[1], grads[3]])
        return block_out, signal_grad, conv_grad, grads[0].T

    earlier = passed_along(hidden_grad, "seq", stride)
    later = passed_along(hidden_grad, "seq", -stride)

    grad_scale = 1.0 / math.sqrt(local_bins * devices)
    block_out = (signal_f + dot(gated, output_weight, ((1,), (0,)))).astype(jnp.bfloat16)
    output_term = dot(gated, cotangent, ((0,), (0,))) * grad_scale
    middle_term = dot(activated, hidden_grad, ((0,), (0,))) * grad_scale
    output_grad, middle_grad = lax.psum((output_term, middle_term), "seq")
    first_term = dot(activated, later, ((0,), (0,))) * grad_scale
    last_term = dot(activated, earlier, ((0,), (0,))) * grad_scale
    first_grad, last_grad = lax.psum((first_term, last_term), "seq")
    conv_grad = jnp.stack([first_grad, middle_grad, last_grad])

    input_gradient = (
        dot(hidden_grad, conv_weight[1], ((1,), (1,)))
        + dot(later, conv_weight[0], ((1,), (1,)))
        + dot(earlier, conv_weight[2], ((1,), (1,)))
    )
    weighted = input_gradient * gelu_slope(normed, normed_cdf) * norm_gain
    inner = jnp.mean(weighted * signal_f, axis=-1, keepdims=True)
    cubed = inverse_rms * inverse_rms * inverse_rms
    signal_grad = cotangent.astype(jnp.float32) + weighted * inverse_rms - signal_f * cubed * inner
    return (block_out, signal_grad.astype(jnp.bfloat16), conv_grad, output_grad)


def solution(mesh):
    placed = (P(("groups", "seq"), None), P(), P(), P(), P(("groups", "seq"), None))
    return jax.shard_map(
        shards,
        mesh=mesh,
        in_specs=placed,
        out_specs=(
            P(("groups", "seq"), None),
            P(("groups", "seq"), None),
            P("groups", None, None),
            P("groups", None),
        ),
        check_vma=False,
    )
```

```python
import functools
import math

import jax
import jax.numpy as jnp
from jax import lax
from jax.experimental import pallas as pl
from jax.experimental.pallas import tpu as pltpu
from jax.sharding import PartitionSpec as P

epsilon = 1e-06


def passed_along(block, axis, distance):
    devices = range(lax.axis_size(axis))
    route = [(i - distance, i) for i in devices if i - distance in devices]
    return lax.ppermute(block, axis, route)


def gelu_cdf(value):
    return 0.5 * (1.0 + jax.scipy.special.erf(value * (1.0 / math.sqrt(2.0))))


def gelu_slope(value, cdf):
    return cdf + value * jnp.exp(-0.5 * value * value) * (1.0 / math.sqrt(2.0 * math.pi))


def dot(left, right, contract):
    return lax.dot_general(left, right, (contract, ((), ())), preferred_element_type=jnp.float32)


def whole_block(
    devices, signal, cotangent, conv_weight, output_weight, norm_gain,
    block_out, signal_grad, grads, output_grad,
    activated, hidden, gated_grad, gated, hidden_grad,
    far_out, far_in, near_out, near_in, earlier, later,
    mine, from_sibling, half, pieces,
    far_send, far_recv, near_send, near_recv, up_send, up_recv, down_send, down_recv,
    pair_send, pair_recv, scatter_send, scatter_recv,
    gather_send, gather_recv, back_send, back_recv,
):
    stride = devices // 8
    chips = devices // 2
    channels, width = conv_weight.shape[1:]
    bins = signal.shape[0]
    piece = channels // chips
    grad_scale = 1.0 / math.sqrt(bins * devices)
    me = lax.axis_index("seq")
    chip, core = me // 2, me % 2
    sibling = chip * 2 + 1 - core
    odd = lax.rem(me // stride, 2)
    step_sign = 2 * odd - 1
    far_tap, near_tap = 2 - 2 * odd, 2 * odd
    tile = 256
    chunks = bins // tile

    def wrapped(device):
        return {"seq": lax.rem(device + devices, devices)}

    def peer(distance):
        other = lax.rem(chip + distance, chips)
        return other, {"seq": other * 2 + core}

    def rows(step):
        return pl.ds(pl.multiple_of(step * tile, tile), tile)

    barrier = pltpu.get_barrier_semaphore()
    pl.semaphore_signal(barrier, inc=1, device_id={"seq": sibling})
    for distance in range(1, chips):
        pl.semaphore_signal(barrier, inc=1, device_id=peer(distance)[1])
    pl.semaphore_wait(barrier, chips)

    far_target = me + 2 * stride * step_sign
    far_source = me - 2 * stride * step_sign
    sends_far = jnp.logical_and(far_target >= 0, far_target < devices)
    takes_far = jnp.logical_and(far_source >= 0, far_source < devices)
    has_after, has_before = me + stride < devices, me >= stride

    def far_copy(step):
        at = rows(step)
        return pltpu.make_async_remote_copy(
            far_out.at[at], far_in.at[at], far_send.at[step], far_recv.at[step],
            device_id=wrapped(far_target),
        )

    def near_copy(step):
        at = rows(step)
        return pltpu.make_async_remote_copy(
            near_out.at[at], near_in.at[at], near_send.at[step], near_recv.at[step],
            device_id=wrapped(me - stride * step_sign),
        )

    def up_copy(step):
        at = rows(step)
        return pltpu.make_async_remote_copy(
            hidden_grad.at[at], earlier.at[at], up_send.at[step], up_recv.at[step],
            device_id=wrapped(me + stride),
        )

    def down_copy(step):
        at = rows(step)
        return pltpu.make_async_remote_copy(
            hidden_grad.at[at], later.at[at], down_send.at[step], down_recv.at[step],
            device_id=wrapped(me - stride),
        )

    @pl.when(jnp.logical_not(has_before))
    def _():
        earlier[...] = jnp.zeros_like(earlier)

    @pl.when(jnp.logical_not(has_after))
    def _():
        later[...] = jnp.zeros_like(later)

    @pl.when(jnp.logical_not(takes_far))
    def _():
        far_in[...] = jnp.zeros_like(far_in)

    def normalized(at):
        signal_f = signal[at, :].astype(jnp.float32)
        mean_square = jnp.mean(signal_f * signal_f, axis=-1, keepdims=True)
        inverse_rms = lax.rsqrt(mean_square + epsilon)
        return signal_f, inverse_rms, signal_f * inverse_rms * norm_gain[...]

    @pl.loop(0, chunks)
    def _(step):
        at = rows(step)
        _, _, normed = normalized(at)
        block = (normed * gelu_cdf(normed)).astype(jnp.bfloat16)
        activated[at, :] = block
        far_out[at, :] = dot(block, conv_weight[far_tap], ((1,), (0,))).astype(jnp.bfloat16)
        pl.when(sends_far)(far_copy(step).start)

    @pl.loop(0, chunks)
    def _(step):
        at = rows(step)
        pl.when(takes_far)(far_copy(step).wait_recv)
        block = activated[at, :]
        near = dot(block, conv_weight[near_tap], ((1,), (0,))) + far_in[at, :].astype(jnp.float32)
        near_out[at, :] = near.astype(jnp.bfloat16)
        near_copy(step).start()
        hidden[at, :] = dot(block, conv_weight[1], ((1,), (0,)))
        gated_grad[at, :] = dot(cotangent[at, :], output_weight[...], ((1,), (1,)))

    @pl.loop(0, chunks)
    def _(step):
        at = rows(step)
        near_copy(step).wait_recv()
        value = hidden[at, :] + near_in[at, :].astype(jnp.float32)
        cdf = gelu_cdf(value)
        hidden_grad[at, :] = (gated_grad[at, :] * gelu_slope(value, cdf)).astype(jnp.bfloat16)
        pl.when(has_after)(up_copy(step).start)
        pl.when(has_before)(down_copy(step).start)
        gated[at, :] = (value * cdf).astype(jnp.bfloat16)

    def part(batch, side):
        return 3 - 2 * side if batch == 0 else 2 * side

    def contribution(index, left, right):
        @pl.loop(0, channels // tile)
        def _(step):
            at = rows(step)
            mine[index, at, :] = dot(left[:, at], right[...], ((0,), (0,))).astype(jnp.bfloat16)

    def start_pair(batch):
        copy = pltpu.make_async_remote_copy(
            mine.at[part(batch, 1 - core)], from_sibling.at[batch],
            pair_send.at[batch], pair_recv.at[batch], device_id={"seq": sibling},
        )
        copy.start()
        return copy

    def start_scatter(batch):
        half[batch] = (
            mine[part(batch, core)].astype(jnp.float32) + from_sibling[batch].astype(jnp.float32)
        ).astype(jnp.bfloat16)
        copies = []
        for distance in range(1, chips):
            other, device = peer(distance)
            copy = pltpu.make_async_remote_copy(
                half.at[batch, pl.ds(pl.multiple_of(other * piece, piece), piece)],
                pieces.at[batch, distance - 1],
                scatter_send.at[batch, distance - 1], scatter_recv.at[batch, distance - 1],
                device_id=device,
            )
            copy.start()
            copies.append(copy)
        return copies

    def start_gather(batch):
        index = part(batch, core)
        at = pl.ds(pl.multiple_of(chip * piece, piece), piece)
        total = half[batch, at, :].astype(jnp.float32)
        for distance in range(1, chips):
            total = total + pieces[batch, distance - 1].astype(jnp.float32)
        grads[index, at, :] = total.astype(jnp.bfloat16)
        copies = []
        for distance in range(1, chips):
            copy = pltpu.make_async_remote_copy(
                grads.at[index, at], grads.at[index, at],
                gather_send.at[batch, distance - 1], gather_recv.at[batch, distance - 1],
                device_id=peer(distance)[1],
            )
            copy.start()
            copies.append(copy)
        return copies

    def start_back(batch):
        index = part(batch, core)
        copy = pltpu.make_async_remote_copy(
            grads.at[index], grads.at[index],
            back_send.at[batch], back_recv.at[batch], device_id={"seq": sibling},
        )
        copy.start()
        return copy

    contribution(3, cotangent, gated)
    contribution(1, activated, hidden_grad)
    pair0 = start_pair(0)

    @pl.loop(0, chunks)
    def _(step):
        at = rows(step)
        block_out[at, :] = (
            signal[at, :].astype(jnp.float32)
            + dot(gated[at, :], output_weight[...], ((1,), (0,)))
        ).astype(jnp.bfloat16)

    pair0.wait_recv()
    scatter0 = start_scatter(0)

    @pl.loop(0, chunks)
    def _(step):
        pl.when(has_after)(down_copy(step).wait_recv)
        pl.when(has_before)(up_copy(step).wait_recv)

    contribution(0, activated, later)
    contribution(2, activated, earlier)
    pair1 = start_pair(1)
    for copy in scatter0:
        copy.wait_recv()
    gather0 = start_gather(0)
    pair1.wait_recv()
    scatter1 = start_scatter(1)

    @pl.loop(0, chunks)
    def _(step):
        at = rows(step)
        signal_f, inverse_rms, normed = normalized(at)
        input_gradient = (
            dot(hidden_grad[at, :], conv_weight[1], ((1,), (1,)))
            + dot(later[at, :], conv_weight[0], ((1,), (1,)))
            + dot(earlier[at, :], conv_weight[2], ((1,), (1,)))
        )
        weighted = input_gradient * gelu_slope(normed, gelu_cdf(normed)) * norm_gain[...]
        inner = jnp.mean(weighted * signal_f, axis=-1, keepdims=True)
        cubed = inverse_rms * inverse_rms * inverse_rms
        signal_grad[at, :] = (
            cotangent[at, :].astype(jnp.float32)
            + weighted * inverse_rms
            - signal_f * cubed * inner
        ).astype(jnp.bfloat16)

    for copy in gather0:
        copy.wait_recv()
    back0 = start_back(0)
    for copy in scatter1:
        copy.wait_recv()
    gather1 = start_gather(1)
    back0.wait_recv()
    output_grad[...] = grads[3].astype(jnp.float32).T * grad_scale
    for copy in gather1:
        copy.wait_recv()
    back1 = start_back(1)
    back1.wait_recv()
    for copy in [pair0, pair1, back0, back1] + scatter0 + scatter1 + gather0 + gather1:
        copy.wait_send()

    @pl.loop(0, chunks)
    def _(step):
        near_copy(step).wait_send()
        pl.when(sends_far)(far_copy(step).wait_send)
        pl.when(has_after)(up_copy(step).wait_send)
        pl.when(has_before)(down_copy(step).wait_send)


def run_whole_block(signal, norm_gain, conv_weight, output_weight, cotangent):
    devices = lax.axis_size("seq")
    chips = devices // 2
    bins, channels = signal.shape
    width = output_weight.shape[0]
    chunks = bins // 256
    bf16, f32 = jnp.bfloat16, jnp.float32
    vmem = pl.BlockSpec(memory_space=pltpu.VMEM)
    dma = pltpu.SemaphoreType.DMA
    narrow = pltpu.VMEM((bins, width), bf16)
    wide = pltpu.VMEM((bins, width), f32)
    return pl.pallas_call(
        functools.partial(whole_block, devices),
        out_shape=(
            jax.ShapeDtypeStruct((bins, channels), bf16),
            jax.ShapeDtypeStruct((bins, channels), bf16),
            jax.ShapeDtypeStruct((4, channels, width), bf16),
            jax.ShapeDtypeStruct((width, channels), f32),
        ),
        in_specs=[vmem] * 5,
        out_specs=(vmem,) * 4,
        scratch_shapes=[
            pltpu.VMEM((bins, channels), bf16), wide, wide, narrow, narrow,
            narrow, narrow, narrow, narrow, narrow, narrow,
            pltpu.VMEM((4, channels, width), bf16),
            pltpu.VMEM((2, channels, width), bf16),
            pltpu.VMEM((2, channels, width), bf16),
            pltpu.VMEM((2, chips - 1, channels // chips, width), bf16),
        ]
        + [dma((chunks,))] * 8
        + [dma((2,))] * 2
        + [dma((2, chips - 1))] * 4
        + [dma((2,))] * 2,
        compiler_params=pltpu.CompilerParams(
            collective_id=0, has_side_effects=True, vmem_limit_bytes=48 << 20
        ),
        name="whole_block",
    )(signal, cotangent, conv_weight, output_weight, norm_gain.reshape(1, -1))


def shards(signal, norm_gain, conv_weight, output_weight, cotangent):
    devices = lax.axis_size("seq")
    stride = devices // 8
    local_bins = signal.shape[0]
    if devices == 16:
        block_out, signal_grad, grads, output_grad = run_whole_block(
            signal, norm_gain, conv_weight, output_weight, cotangent
        )
        conv_grad = grads[:3].astype(jnp.float32) * (1.0 / math.sqrt(local_bins * devices))
        return block_out, signal_grad, conv_grad, output_grad
    odd = (lax.axis_index("seq") // stride) % 2 == 1
    far_weight = jnp.where(odd, conv_weight[0], conv_weight[2])
    near_weight = jnp.where(odd, conv_weight[2], conv_weight[0])
    far_route, near_route = [], []
    for i in range(devices):
        is_odd = (i // stride) % 2 == 1
        target = i + 2 * stride if is_odd else i - 2 * stride
        if 0 <= target < devices:
            far_route.append((i, target))
        near_route.append((i, i - stride if is_odd else i + stride))

    signal_f = signal.astype(jnp.float32)
    mean_square = jnp.mean(signal_f * signal_f, axis=-1, keepdims=True)
    inverse_rms = lax.rsqrt(mean_square + epsilon)
    normed = signal_f * inverse_rms * norm_gain
    normed_cdf = gelu_cdf(normed)
    activated = (normed * normed_cdf).astype(jnp.bfloat16)

    chunks = 2
    rows = local_bins // chunks
    parts = []
    for j in range(chunks):
        block = activated[j * rows : (j + 1) * rows]
        far = dot(block, far_weight, ((1,), (0,))).astype(jnp.bfloat16)
        parts.append(lax.ppermute(far, "seq", far_route))
    arrived = []
    for j in range(chunks):
        block = activated[j * rows : (j + 1) * rows]
        near = dot(block, near_weight, ((1,), (0,))) + parts[j].astype(jnp.float32)
        arrived.append(lax.ppermute(near.astype(jnp.bfloat16), "seq", near_route))
    hidden = dot(activated, conv_weight[1], ((1,), (0,))) + jnp.concatenate(arrived).astype(
        jnp.float32
    )
    hidden_cdf = gelu_cdf(hidden)
    gated = (hidden * hidden_cdf).astype(jnp.bfloat16)
    gated_grad = dot(cotangent, output_weight, ((1,), (1,)))
    hidden_grad = (gated_grad * gelu_slope(hidden, hidden_cdf)).astype(jnp.bfloat16)
    earlier = passed_along(hidden_grad, "seq", stride)
    later = passed_along(hidden_grad, "seq", -stride)

    grad_scale = 1.0 / math.sqrt(local_bins * devices)
    block_out = (signal_f + dot(gated, output_weight, ((1,), (0,)))).astype(jnp.bfloat16)
    output_term = dot(gated, cotangent, ((0,), (0,))) * grad_scale
    middle_term = dot(activated, hidden_grad, ((0,), (0,))) * grad_scale
    output_grad, middle_grad = lax.psum((output_term, middle_term), "seq")
    first_term = dot(activated, later, ((0,), (0,))) * grad_scale
    last_term = dot(activated, earlier, ((0,), (0,))) * grad_scale
    first_grad, last_grad = lax.psum((first_term, last_term), "seq")
    conv_grad = jnp.stack([first_grad, middle_grad, last_grad])

    input_gradient = (
        dot(hidden_grad, conv_weight[1], ((1,), (1,)))
        + dot(later, conv_weight[0], ((1,), (1,)))
        + dot(earlier, conv_weight[2], ((1,), (1,)))
    )
    weighted = input_gradient * gelu_slope(normed, normed_cdf) * norm_gain
    inner = jnp.mean(weighted * signal_f, axis=-1, keepdims=True)
    cubed = inverse_rms * inverse_rms * inverse_rms
    signal_grad = cotangent.astype(jnp.float32) + weighted * inverse_rms - signal_f * cubed * inner
    return (block_out, signal_grad.astype(jnp.bfloat16), conv_grad, output_grad)


def solution(mesh):
    placed = (P(("groups", "seq"), None), P(), P(), P(), P(("groups", "seq"), None))
    return jax.shard_map(
        shards,
        mesh=mesh,
        in_specs=placed,
        out_specs=(
            P(("groups", "seq"), None),
            P(("groups", "seq"), None),
            P("groups", None, None),
            P("groups", None),
        ),
        check_vma=False,
    )
```

```python
import functools
import math

import jax
import jax.numpy as jnp
from jax import lax
from jax.experimental import pallas as pl
from jax.experimental.pallas import tpu as pltpu
from jax.sharding import PartitionSpec as P

epsilon = 1e-06


def passed_along(block, axis, distance):
    devices = range(lax.axis_size(axis))
    route = [(i - distance, i) for i in devices if i - distance in devices]
    return lax.ppermute(block, axis, route)


def gelu_cdf(value):
    return 0.5 * (1.0 + jax.scipy.special.erf(value * (1.0 / math.sqrt(2.0))))


def gelu_slope(value, cdf):
    return cdf + value * jnp.exp(-0.5 * value * value) * (1.0 / math.sqrt(2.0 * math.pi))


def dot(left, right, contract):
    return lax.dot_general(left, right, (contract, ((), ())), preferred_element_type=jnp.float32)


def whole_block(
    devices, signal, cotangent, conv_weight, output_weight, norm_gain,
    block_out, signal_grad, grads, output_grad,
    activated, transposed, hidden, gated_grad, gated, hidden_grad,
    far_out, far_in, near_out, near_in, earlier, later,
    mine, from_sibling, half, pieces,
    far_send, far_recv, near_send, near_recv, up_send, up_recv, down_send, down_recv,
    pair_send, pair_recv, scatter_send, scatter_recv,
    gather_send, gather_recv, back_send, back_recv,
):
    stride = devices // 8
    chips = devices // 2
    channels, width = conv_weight.shape[1:]
    bins = signal.shape[0]
    piece = channels // chips
    grad_scale = 1.0 / math.sqrt(bins * devices)
    me = lax.axis_index("seq")
    chip, core = me // 2, me % 2
    sibling = chip * 2 + 1 - core
    odd = lax.rem(me // stride, 2)
    step_sign = 2 * odd - 1
    far_tap, near_tap = 2 - 2 * odd, 2 * odd
    tile, chunk = 256, 128
    chunks = bins // chunk

    def wrapped(device):
        return {"seq": lax.rem(device + devices, devices)}

    def peer(distance):
        other = lax.rem(chip + distance, chips)
        return other, {"seq": other * 2 + core}

    def rows(step, size=chunk):
        return pl.ds(pl.multiple_of(step * size, size), size)

    barrier = pltpu.get_barrier_semaphore()
    pl.semaphore_signal(barrier, inc=1, device_id={"seq": sibling})
    for distance in range(1, chips):
        pl.semaphore_signal(barrier, inc=1, device_id=peer(distance)[1])
    pl.semaphore_wait(barrier, chips)

    far_target = me + 2 * stride * step_sign
    far_source = me - 2 * stride * step_sign
    sends_far = jnp.logical_and(far_target >= 0, far_target < devices)
    takes_far = jnp.logical_and(far_source >= 0, far_source < devices)
    has_after, has_before = me + stride < devices, me >= stride

    def far_copy(step):
        at = rows(step)
        return pltpu.make_async_remote_copy(
            far_out.at[at], far_in.at[at], far_send.at[step], far_recv.at[step],
            device_id=wrapped(far_target),
        )

    def near_copy(step):
        at = rows(step)
        return pltpu.make_async_remote_copy(
            near_out.at[at], near_in.at[at], near_send.at[step], near_recv.at[step],
            device_id=wrapped(me - stride * step_sign),
        )

    def up_copy(step):
        at = rows(step)
        return pltpu.make_async_remote_copy(
            hidden_grad.at[at], earlier.at[at], up_send.at[step], up_recv.at[step],
            device_id=wrapped(me + stride),
        )

    def down_copy(step):
        at = rows(step)
        return pltpu.make_async_remote_copy(
            hidden_grad.at[at], later.at[at], down_send.at[step], down_recv.at[step],
            device_id=wrapped(me - stride),
        )

    @pl.when(jnp.logical_not(has_before))
    def _():
        earlier[...] = jnp.zeros_like(earlier)

    @pl.when(jnp.logical_not(has_after))
    def _():
        later[...] = jnp.zeros_like(later)

    @pl.when(jnp.logical_not(takes_far))
    def _():
        far_in[...] = jnp.zeros_like(far_in)

    def normalized(at):
        signal_f = signal[at, :].astype(jnp.float32)
        mean_square = jnp.mean(signal_f * signal_f, axis=-1, keepdims=True)
        inverse_rms = lax.rsqrt(mean_square + epsilon)
        return signal_f, inverse_rms, signal_f * inverse_rms * norm_gain[...]

    @pl.loop(0, chunks)
    def _(step):
        at = rows(step)
        _, _, normed = normalized(at)
        block = (normed * gelu_cdf(normed)).astype(jnp.bfloat16)
        activated[at, :] = block
        far_out[at, :] = dot(block, conv_weight[far_tap], ((1,), (0,))).astype(jnp.bfloat16)
        pl.when(sends_far)(far_copy(step).start)
        hidden[at, :] = dot(block, conv_weight[1], ((1,), (0,)))
        gated_grad[at, :] = dot(cotangent[at, :], output_weight[...], ((1,), (1,)))

    @pl.loop(0, chunks)
    def _(step):
        at = rows(step)
        pl.when(takes_far)(far_copy(step).wait_recv)
        near = dot(activated[at, :], conv_weight[near_tap], ((1,), (0,))) + far_in[at, :].astype(jnp.float32)
        near_out[at, :] = near.astype(jnp.bfloat16)
        near_copy(step).start()

    @pl.loop(0, chunks)
    def _(step):
        at = rows(step)
        near_copy(step).wait_recv()
        value = hidden[at, :] + near_in[at, :].astype(jnp.float32)
        cdf = gelu_cdf(value)
        hidden_grad[at, :] = (gated_grad[at, :] * gelu_slope(value, cdf)).astype(jnp.bfloat16)
        pl.when(has_after)(up_copy(step).start)
        pl.when(has_before)(down_copy(step).start)
        gated[at, :] = (value * cdf).astype(jnp.bfloat16)

    def part(batch, side):
        return 3 - 2 * side if batch == 0 else 2 * side

    def contribution(index, right):
        @pl.loop(0, channels // tile)
        def _(step):
            at = rows(step, tile)
            mine[index, at, :] = dot(transposed[at, :], right[...], ((1,), (0,))).astype(
                jnp.bfloat16
            )

    def start_pair(batch):
        copy = pltpu.make_async_remote_copy(
            mine.at[part(batch, 1 - core)], from_sibling.at[batch],
            pair_send.at[batch], pair_recv.at[batch], device_id={"seq": sibling},
        )
        copy.start()
        return copy

    def start_scatter(batch):
        half[batch] = (
            mine[part(batch, core)].astype(jnp.float32) + from_sibling[batch].astype(jnp.float32)
        ).astype(jnp.bfloat16)
        copies = []
        for distance in range(1, chips):
            other, device = peer(distance)
            copy = pltpu.make_async_remote_copy(
                half.at[batch, pl.ds(pl.multiple_of(other * piece, piece), piece)],
                pieces.at[batch, distance - 1],
                scatter_send.at[batch, distance - 1], scatter_recv.at[batch, distance - 1],
                device_id=device,
            )
            copy.start()
            copies.append(copy)
        return copies

    def start_gather(batch):
        index = part(batch, core)
        at = pl.ds(pl.multiple_of(chip * piece, piece), piece)
        total = half[batch, at, :].astype(jnp.float32)
        for distance in range(1, chips):
            total = total + pieces[batch, distance - 1].astype(jnp.float32)
        grads[index, at, :] = total.astype(jnp.bfloat16)
        copies = []
        for distance in range(1, chips):
            copy = pltpu.make_async_remote_copy(
                grads.at[index, at], grads.at[index, at],
                gather_send.at[batch, distance - 1], gather_recv.at[batch, distance - 1],
                device_id=peer(distance)[1],
            )
            copy.start()
            copies.append(copy)
        return copies

    def start_back(batch):
        index = part(batch, core)
        copy = pltpu.make_async_remote_copy(
            grads.at[index], grads.at[index],
            back_send.at[batch], back_recv.at[batch], device_id={"seq": sibling},
        )
        copy.start()
        return copy

    @pl.loop(0, channels // tile)
    def _(step):
        at = rows(step, tile)
        mine[3, at, :] = dot(cotangent[:, at], gated[...], ((0,), (0,))).astype(jnp.bfloat16)
        transposed[at, :] = activated[:, at].T

    contribution(1, hidden_grad)
    pair0 = start_pair(0)
    pair0.wait_recv()
    scatter0 = start_scatter(0)

    @pl.loop(0, bins // tile)
    def _(step):
        at = rows(step, tile)
        block_out[at, :] = (
            signal[at, :].astype(jnp.float32)
            + dot(gated[at, :], output_weight[...], ((1,), (0,)))
        ).astype(jnp.bfloat16)

    for copy in scatter0:
        copy.wait_recv()
    gather0 = start_gather(0)

    @pl.loop(0, chunks)
    def _(step):
        pl.when(has_after)(down_copy(step).wait_recv)
        pl.when(has_before)(up_copy(step).wait_recv)

    contribution(0, later)
    contribution(2, earlier)
    pair1 = start_pair(1)
    pair1.wait_recv()
    scatter1 = start_scatter(1)

    @pl.loop(0, bins // tile)
    def _(step):
        at = rows(step, tile)
        signal_f, inverse_rms, normed = normalized(at)
        input_gradient = (
            dot(hidden_grad[at, :], conv_weight[1], ((1,), (1,)))
            + dot(later[at, :], conv_weight[0], ((1,), (1,)))
            + dot(earlier[at, :], conv_weight[2], ((1,), (1,)))
        )
        weighted = input_gradient * gelu_slope(normed, gelu_cdf(normed)) * norm_gain[...]
        inner = jnp.mean(weighted * signal_f, axis=-1, keepdims=True)
        cubed = inverse_rms * inverse_rms * inverse_rms
        signal_grad[at, :] = (
            cotangent[at, :].astype(jnp.float32)
            + weighted * inverse_rms
            - signal_f * cubed * inner
        ).astype(jnp.bfloat16)

    for copy in gather0:
        copy.wait_recv()
    back0 = start_back(0)
    for copy in scatter1:
        copy.wait_recv()
    gather1 = start_gather(1)
    back0.wait_recv()
    output_grad[...] = grads[3].astype(jnp.float32).T * grad_scale
    for copy in gather1:
        copy.wait_recv()
    back1 = start_back(1)
    back1.wait_recv()
    for copy in [pair0, pair1, back0, back1] + scatter0 + scatter1 + gather0 + gather1:
        copy.wait_send()

    @pl.loop(0, chunks)
    def _(step):
        near_copy(step).wait_send()
        pl.when(sends_far)(far_copy(step).wait_send)
        pl.when(has_after)(up_copy(step).wait_send)
        pl.when(has_before)(down_copy(step).wait_send)


def run_whole_block(signal, norm_gain, conv_weight, output_weight, cotangent):
    devices = lax.axis_size("seq")
    chips = devices // 2
    bins, channels = signal.shape
    width = output_weight.shape[0]
    chunks = bins // 128
    bf16, f32 = jnp.bfloat16, jnp.float32
    vmem = pl.BlockSpec(memory_space=pltpu.VMEM)
    dma = pltpu.SemaphoreType.DMA
    narrow = pltpu.VMEM((bins, width), bf16)
    wide = pltpu.VMEM((bins, width), f32)
    return pl.pallas_call(
        functools.partial(whole_block, devices),
        out_shape=(
            jax.ShapeDtypeStruct((bins, channels), bf16),
            jax.ShapeDtypeStruct((bins, channels), bf16),
            jax.ShapeDtypeStruct((4, channels, width), bf16),
            jax.ShapeDtypeStruct((width, channels), f32),
        ),
        in_specs=[vmem] * 5,
        out_specs=(vmem,) * 4,
        scratch_shapes=[
            pltpu.VMEM((bins, channels), bf16), pltpu.VMEM((channels, bins), bf16),
            wide, wide, narrow, narrow,
            narrow, narrow, narrow, narrow, narrow, narrow,
            pltpu.VMEM((4, channels, width), bf16),
            pltpu.VMEM((2, channels, width), bf16),
            pltpu.VMEM((2, channels, width), bf16),
            pltpu.VMEM((2, chips - 1, channels // chips, width), bf16),
        ]
        + [dma((chunks,))] * 8
        + [dma((2,))] * 2
        + [dma((2, chips - 1))] * 4
        + [dma((2,))] * 2,
        compiler_params=pltpu.CompilerParams(
            collective_id=0, has_side_effects=True, vmem_limit_bytes=48 << 20
        ),
        name="whole_block",
    )(signal, cotangent, conv_weight, output_weight, norm_gain.reshape(1, -1))


def shards(signal, norm_gain, conv_weight, output_weight, cotangent):
    devices = lax.axis_size("seq")
    stride = devices // 8
    local_bins = signal.shape[0]
    if devices == 16:
        block_out, signal_grad, grads, output_grad = run_whole_block(
            signal, norm_gain, conv_weight, output_weight, cotangent
        )
        conv_grad = grads[:3].astype(jnp.float32) * (1.0 / math.sqrt(local_bins * devices))
        return block_out, signal_grad, conv_grad, output_grad
    odd = (lax.axis_index("seq") // stride) % 2 == 1
    far_weight = jnp.where(odd, conv_weight[0], conv_weight[2])
    near_weight = jnp.where(odd, conv_weight[2], conv_weight[0])
    far_route, near_route = [], []
    for i in range(devices):
        is_odd = (i // stride) % 2 == 1
        target = i + 2 * stride if is_odd else i - 2 * stride
        if 0 <= target < devices:
            far_route.append((i, target))
        near_route.append((i, i - stride if is_odd else i + stride))

    signal_f = signal.astype(jnp.float32)
    mean_square = jnp.mean(signal_f * signal_f, axis=-1, keepdims=True)
    inverse_rms = lax.rsqrt(mean_square + epsilon)
    normed = signal_f * inverse_rms * norm_gain
    normed_cdf = gelu_cdf(normed)
    activated = (normed * normed_cdf).astype(jnp.bfloat16)

    chunks = 2
    rows = local_bins // chunks
    parts = []
    for j in range(chunks):
        block = activated[j * rows : (j + 1) * rows]
        far = dot(block, far_weight, ((1,), (0,))).astype(jnp.bfloat16)
        parts.append(lax.ppermute(far, "seq", far_route))
    arrived = []
    for j in range(chunks):
        block = activated[j * rows : (j + 1) * rows]
        near = dot(block, near_weight, ((1,), (0,))) + parts[j].astype(jnp.float32)
        arrived.append(lax.ppermute(near.astype(jnp.bfloat16), "seq", near_route))
    hidden = dot(activated, conv_weight[1], ((1,), (0,))) + jnp.concatenate(arrived).astype(
        jnp.float32
    )
    hidden_cdf = gelu_cdf(hidden)
    gated = (hidden * hidden_cdf).astype(jnp.bfloat16)
    gated_grad = dot(cotangent, output_weight, ((1,), (1,)))
    hidden_grad = (gated_grad * gelu_slope(hidden, hidden_cdf)).astype(jnp.bfloat16)
    earlier = passed_along(hidden_grad, "seq", stride)
    later = passed_along(hidden_grad, "seq", -stride)

    grad_scale = 1.0 / math.sqrt(local_bins * devices)
    block_out = (signal_f + dot(gated, output_weight, ((1,), (0,)))).astype(jnp.bfloat16)
    output_term = dot(gated, cotangent, ((0,), (0,))) * grad_scale
    middle_term = dot(activated, hidden_grad, ((0,), (0,))) * grad_scale
    output_grad, middle_grad = lax.psum((output_term, middle_term), "seq")
    first_term = dot(activated, later, ((0,), (0,))) * grad_scale
    last_term = dot(activated, earlier, ((0,), (0,))) * grad_scale
    first_grad, last_grad = lax.psum((first_term, last_term), "seq")
    conv_grad = jnp.stack([first_grad, middle_grad, last_grad])

    input_gradient = (
        dot(hidden_grad, conv_weight[1], ((1,), (1,)))
        + dot(later, conv_weight[0], ((1,), (1,)))
        + dot(earlier, conv_weight[2], ((1,), (1,)))
    )
    weighted = input_gradient * gelu_slope(normed, normed_cdf) * norm_gain
    inner = jnp.mean(weighted * signal_f, axis=-1, keepdims=True)
    cubed = inverse_rms * inverse_rms * inverse_rms
    signal_grad = cotangent.astype(jnp.float32) + weighted * inverse_rms - signal_f * cubed * inner
    return (block_out, signal_grad.astype(jnp.bfloat16), conv_grad, output_grad)


def solution(mesh):
    placed = (P(("groups", "seq"), None), P(), P(), P(), P(("groups", "seq"), None))
    return jax.shard_map(
        shards,
        mesh=mesh,
        in_specs=placed,
        out_specs=(
            P(("groups", "seq"), None),
            P(("groups", "seq"), None),
            P("groups", None, None),
            P("groups", None),
        ),
        check_vma=False,
    )
```

```python
import functools
import math

import jax
import jax.numpy as jnp
from jax import lax
from jax.experimental import pallas as pl
from jax.experimental.pallas import tpu as pltpu
from jax.sharding import PartitionSpec as P

epsilon = 1e-06


def passed_along(block, axis, distance):
    devices = range(lax.axis_size(axis))
    route = [(i - distance, i) for i in devices if i - distance in devices]
    return lax.ppermute(block, axis, route)


def gelu_cdf(value):
    return 0.5 * (1.0 + jax.scipy.special.erf(value * (1.0 / math.sqrt(2.0))))


def gelu_slope(value, cdf):
    return cdf + value * jnp.exp(-0.5 * value * value) * (1.0 / math.sqrt(2.0 * math.pi))


def dot(left, right, contract):
    return lax.dot_general(left, right, (contract, ((), ())), preferred_element_type=jnp.float32)


def whole_block(
    devices, signal, cotangent, conv_weight, output_weight, norm_gain,
    block_out, signal_grad, grads, output_grad,
    activated, transposed, hidden, gated_grad, gated, hidden_grad,
    far_out, far_in, near_out, near_in, earlier, later,
    mine, from_sibling, half, pieces,
    far_send, far_recv, near_send, near_recv, up_send, up_recv, down_send, down_recv,
    pair_send, pair_recv, scatter_send, scatter_recv,
    gather_send, gather_recv, back_send, back_recv,
):
    stride = devices // 8
    chips = devices // 2
    channels, width = conv_weight.shape[1:]
    bins = signal.shape[0]
    piece = channels // chips
    grad_scale = 1.0 / math.sqrt(bins * devices)
    me = lax.axis_index("seq")
    chip, core = me // 2, me % 2
    sibling = chip * 2 + 1 - core
    partner = {"seq": (chip + 1 - 2 * lax.rem(chip, 2)) * 2 + core}
    odd = lax.rem(me // stride, 2)
    step_sign = 2 * odd - 1
    far_tap, near_tap = 2 - 2 * odd, 2 * odd
    tile, chunk = 256, 128
    chunks = bins // chunk

    def wrapped(device):
        return {"seq": lax.rem(device + devices, devices)}

    def peer(distance):
        other = lax.rem(chip + distance, chips)
        return other, {"seq": other * 2 + core}

    def rows(step, size=chunk):
        return pl.ds(pl.multiple_of(step * size, size), size)

    barrier = pltpu.get_barrier_semaphore()
    pl.semaphore_signal(barrier, inc=1, device_id={"seq": sibling})
    for distance in range(1, chips):
        pl.semaphore_signal(barrier, inc=1, device_id=peer(distance)[1])
    pl.semaphore_wait(barrier, chips)

    far_target = me + 2 * stride * step_sign
    far_source = me - 2 * stride * step_sign
    sends_far = jnp.logical_and(far_target >= 0, far_target < devices)
    takes_far = jnp.logical_and(far_source >= 0, far_source < devices)
    has_after, has_before = me + stride < devices, me >= stride

    def far_copy(step):
        at = rows(step)
        return pltpu.make_async_remote_copy(
            far_out.at[at], far_in.at[at], far_send.at[step], far_recv.at[step],
            device_id=wrapped(far_target),
        )

    def near_copy(step):
        at = rows(step)
        return pltpu.make_async_remote_copy(
            near_out.at[at], near_in.at[at], near_send.at[step], near_recv.at[step],
            device_id=wrapped(me - stride * step_sign),
        )

    def up_copy(step):
        at = rows(step)
        return pltpu.make_async_remote_copy(
            hidden_grad.at[at], earlier.at[at], up_send.at[step], up_recv.at[step],
            device_id=wrapped(me + stride),
        )

    def down_copy(step):
        at = rows(step)
        return pltpu.make_async_remote_copy(
            hidden_grad.at[at], later.at[at], down_send.at[step], down_recv.at[step],
            device_id=wrapped(me - stride),
        )

    @pl.when(jnp.logical_not(has_before))
    def _():
        earlier[...] = jnp.zeros_like(earlier)

    @pl.when(jnp.logical_not(has_after))
    def _():
        later[...] = jnp.zeros_like(later)

    @pl.when(jnp.logical_not(takes_far))
    def _():
        far_in[...] = jnp.zeros_like(far_in)

    def normalized(at):
        signal_f = signal[at, :].astype(jnp.float32)
        mean_square = jnp.mean(signal_f * signal_f, axis=-1, keepdims=True)
        inverse_rms = lax.rsqrt(mean_square + epsilon)
        return signal_f, inverse_rms, signal_f * inverse_rms * norm_gain[...]

    @pl.loop(0, chunks)
    def _(step):
        at = rows(step)
        _, _, normed = normalized(at)
        block = (normed * gelu_cdf(normed)).astype(jnp.bfloat16)
        activated[at, :] = block
        far_out[at, :] = dot(block, conv_weight[far_tap], ((1,), (0,))).astype(jnp.bfloat16)
        pl.when(sends_far)(far_copy(step).start)
        hidden[at, :] = dot(block, conv_weight[1], ((1,), (0,)))
        gated_grad[at, :] = dot(cotangent[at, :], output_weight[...], ((1,), (1,)))

    @pl.loop(0, chunks)
    def _(step):
        at = rows(step)
        pl.when(takes_far)(far_copy(step).wait_recv)
        near = dot(activated[at, :], conv_weight[near_tap], ((1,), (0,))) + far_in[at, :].astype(jnp.float32)
        near_out[at, :] = near.astype(jnp.bfloat16)
        near_copy(step).start()

    @pl.loop(0, chunks)
    def _(step):
        at = rows(step)
        near_copy(step).wait_recv()
        value = hidden[at, :] + near_in[at, :].astype(jnp.float32)
        cdf = gelu_cdf(value)
        hidden_grad[at, :] = (gated_grad[at, :] * gelu_slope(value, cdf)).astype(jnp.bfloat16)
        pl.when(has_after)(up_copy(step).start)
        pl.when(has_before)(down_copy(step).start)
        gated[at, :] = (value * cdf).astype(jnp.bfloat16)

    def part(batch, side):
        return 3 - 2 * side if batch == 0 else 2 * side

    def contribution(index, right):
        @pl.loop(0, channels // tile)
        def _(step):
            at = rows(step, tile)
            mine[index, at, :] = dot(transposed[at, :], right[...], ((1,), (0,))).astype(
                jnp.bfloat16
            )

    def start_pair(batch):
        copy = pltpu.make_async_remote_copy(
            mine.at[part(batch, 1 - core)], from_sibling.at[batch],
            pair_send.at[batch], pair_recv.at[batch], device_id={"seq": sibling},
        )
        copy.start()
        return copy

    def start_scatter(batch):
        half[batch] = (
            mine[part(batch, core)].astype(jnp.float32) + from_sibling[batch].astype(jnp.float32)
        ).astype(jnp.bfloat16)
        copies = []
        for distance in range(1, chips):
            other, device = peer(distance)
            copy = pltpu.make_async_remote_copy(
                half.at[batch, pl.ds(pl.multiple_of(other * piece, piece), piece)],
                pieces.at[batch, distance - 1],
                scatter_send.at[batch, distance - 1], scatter_recv.at[batch, distance - 1],
                device_id=device,
            )
            copy.start()
            copies.append(copy)
        return copies

    def start_gather(batch):
        index = part(batch, core)
        at = pl.ds(pl.multiple_of(chip * piece, piece), piece)
        total = half[batch, at, :].astype(jnp.float32)
        for distance in range(1, chips):
            total = total + pieces[batch, distance - 1].astype(jnp.float32)
        grads[index, at, :] = total.astype(jnp.bfloat16)
        hops = [peer(2 * k)[1] for k in range(1, chips // 2)] + [partner]
        copies = []
        for slot, device in enumerate(hops):
            copy = pltpu.make_async_remote_copy(
                grads.at[index, at], grads.at[index, at],
                gather_send.at[batch, slot], gather_recv.at[batch, slot], device_id=device,
            )
            copy.start()
            copies.append(copy)
        return copies

    def pass_on(batch, arriving):
        index = part(batch, core)
        copies = arriving[chips // 2 - 1 :]
        for k in range(1, chips // 2):
            arriving[k - 1].wait_recv()
            other = lax.rem(chip + chips - 2 * k, chips)
            at = pl.ds(pl.multiple_of(other * piece, piece), piece)
            slot = chips // 2 - 1 + k
            copy = pltpu.make_async_remote_copy(
                grads.at[index, at], grads.at[index, at],
                gather_send.at[batch, slot], gather_recv.at[batch, slot], device_id=partner,
            )
            copy.start()
            copies.append(copy)
        return copies

    def start_back(batch):
        index = part(batch, core)
        copy = pltpu.make_async_remote_copy(
            grads.at[index], grads.at[index],
            back_send.at[batch], back_recv.at[batch], device_id={"seq": sibling},
        )
        copy.start()
        return copy

    @pl.loop(0, channels // tile)
    def _(step):
        at = rows(step, tile)
        mine[3, at, :] = dot(cotangent[:, at], gated[...], ((0,), (0,))).astype(jnp.bfloat16)
        transposed[at, :] = activated[:, at].T

    contribution(1, hidden_grad)
    pair0 = start_pair(0)
    pair0.wait_recv()
    scatter0 = start_scatter(0)

    @pl.loop(0, bins // tile)
    def _(step):
        at = rows(step, tile)
        block_out[at, :] = (
            signal[at, :].astype(jnp.float32)
            + dot(gated[at, :], output_weight[...], ((1,), (0,)))
        ).astype(jnp.bfloat16)

    for copy in scatter0:
        copy.wait_recv()
    gather0 = start_gather(0)
    passed0 = pass_on(0, gather0)

    @pl.loop(0, chunks)
    def _(step):
        pl.when(has_after)(down_copy(step).wait_recv)
        pl.when(has_before)(up_copy(step).wait_recv)

    contribution(0, later)
    contribution(2, earlier)
    pair1 = start_pair(1)
    pair1.wait_recv()
    scatter1 = start_scatter(1)

    @pl.loop(0, bins // tile)
    def _(step):
        at = rows(step, tile)
        signal_f, inverse_rms, normed = normalized(at)
        input_gradient = (
            dot(hidden_grad[at, :], conv_weight[1], ((1,), (1,)))
            + dot(later[at, :], conv_weight[0], ((1,), (1,)))
            + dot(earlier[at, :], conv_weight[2], ((1,), (1,)))
        )
        weighted = input_gradient * gelu_slope(normed, gelu_cdf(normed)) * norm_gain[...]
        inner = jnp.mean(weighted * signal_f, axis=-1, keepdims=True)
        cubed = inverse_rms * inverse_rms * inverse_rms
        signal_grad[at, :] = (
            cotangent[at, :].astype(jnp.float32)
            + weighted * inverse_rms
            - signal_f * cubed * inner
        ).astype(jnp.bfloat16)

    for copy in passed0:
        copy.wait_recv()
    back0 = start_back(0)
    for copy in scatter1:
        copy.wait_recv()
    gather1 = start_gather(1)
    passed1 = pass_on(1, gather1)
    back0.wait_recv()
    output_grad[...] = grads[3].astype(jnp.float32).T * grad_scale
    for copy in passed1:
        copy.wait_recv()
    back1 = start_back(1)
    back1.wait_recv()
    for copy in [pair0, pair1, back0, back1] + scatter0 + scatter1:
        copy.wait_send()
    for copy in gather0[:-1] + passed0 + gather1[:-1] + passed1:
        copy.wait_send()

    @pl.loop(0, chunks)
    def _(step):
        near_copy(step).wait_send()
        pl.when(sends_far)(far_copy(step).wait_send)
        pl.when(has_after)(up_copy(step).wait_send)
        pl.when(has_before)(down_copy(step).wait_send)


def run_whole_block(signal, norm_gain, conv_weight, output_weight, cotangent):
    devices = lax.axis_size("seq")
    chips = devices // 2
    bins, channels = signal.shape
    width = output_weight.shape[0]
    chunks = bins // 128
    bf16, f32 = jnp.bfloat16, jnp.float32
    vmem = pl.BlockSpec(memory_space=pltpu.VMEM)
    dma = pltpu.SemaphoreType.DMA
    narrow = pltpu.VMEM((bins, width), bf16)
    wide = pltpu.VMEM((bins, width), f32)
    return pl.pallas_call(
        functools.partial(whole_block, devices),
        out_shape=(
            jax.ShapeDtypeStruct((bins, channels), bf16),
            jax.ShapeDtypeStruct((bins, channels), bf16),
            jax.ShapeDtypeStruct((4, channels, width), bf16),
            jax.ShapeDtypeStruct((width, channels), f32),
        ),
        in_specs=[vmem] * 5,
        out_specs=(vmem,) * 4,
        scratch_shapes=[
            pltpu.VMEM((bins, channels), bf16), pltpu.VMEM((channels, bins), bf16),
            wide, wide, narrow, narrow,
            narrow, narrow, narrow, narrow, narrow, narrow,
            pltpu.VMEM((4, channels, width), bf16),
            pltpu.VMEM((2, channels, width), bf16),
            pltpu.VMEM((2, channels, width), bf16),
            pltpu.VMEM((2, chips - 1, channels // chips, width), bf16),
        ]
        + [dma((chunks,))] * 8
        + [dma((2,))] * 2
        + [dma((2, chips - 1))] * 4
        + [dma((2,))] * 2,
        compiler_params=pltpu.CompilerParams(
            collective_id=0, has_side_effects=True, vmem_limit_bytes=48 << 20
        ),
        name="whole_block",
    )(signal, cotangent, conv_weight, output_weight, norm_gain.reshape(1, -1))


def shards(signal, norm_gain, conv_weight, output_weight, cotangent):
    devices = lax.axis_size("seq")
    stride = devices // 8
    local_bins = signal.shape[0]
    if devices == 16:
        block_out, signal_grad, grads, output_grad = run_whole_block(
            signal, norm_gain, conv_weight, output_weight, cotangent
        )
        conv_grad = grads[:3].astype(jnp.float32) * (1.0 / math.sqrt(local_bins * devices))
        return block_out, signal_grad, conv_grad, output_grad
    odd = (lax.axis_index("seq") // stride) % 2 == 1
    far_weight = jnp.where(odd, conv_weight[0], conv_weight[2])
    near_weight = jnp.where(odd, conv_weight[2], conv_weight[0])
    far_route, near_route = [], []
    for i in range(devices):
        is_odd = (i // stride) % 2 == 1
        target = i + 2 * stride if is_odd else i - 2 * stride
        if 0 <= target < devices:
            far_route.append((i, target))
        near_route.append((i, i - stride if is_odd else i + stride))

    signal_f = signal.astype(jnp.float32)
    mean_square = jnp.mean(signal_f * signal_f, axis=-1, keepdims=True)
    inverse_rms = lax.rsqrt(mean_square + epsilon)
    normed = signal_f * inverse_rms * norm_gain
    normed_cdf = gelu_cdf(normed)
    activated = (normed * normed_cdf).astype(jnp.bfloat16)

    chunks = 2
    rows = local_bins // chunks
    parts = []
    for j in range(chunks):
        block = activated[j * rows : (j + 1) * rows]
        far = dot(block, far_weight, ((1,), (0,))).astype(jnp.bfloat16)
        parts.append(lax.ppermute(far, "seq", far_route))
    arrived = []
    for j in range(chunks):
        block = activated[j * rows : (j + 1) * rows]
        near = dot(block, near_weight, ((1,), (0,))) + parts[j].astype(jnp.float32)
        arrived.append(lax.ppermute(near.astype(jnp.bfloat16), "seq", near_route))
    hidden = dot(activated, conv_weight[1], ((1,), (0,))) + jnp.concatenate(arrived).astype(
        jnp.float32
    )
    hidden_cdf = gelu_cdf(hidden)
    gated = (hidden * hidden_cdf).astype(jnp.bfloat16)
    gated_grad = dot(cotangent, output_weight, ((1,), (1,)))
    hidden_grad = (gated_grad * gelu_slope(hidden, hidden_cdf)).astype(jnp.bfloat16)
    earlier = passed_along(hidden_grad, "seq", stride)
    later = passed_along(hidden_grad, "seq", -stride)

    grad_scale = 1.0 / math.sqrt(local_bins * devices)
    block_out = (signal_f + dot(gated, output_weight, ((1,), (0,)))).astype(jnp.bfloat16)
    output_term = dot(gated, cotangent, ((0,), (0,))) * grad_scale
    middle_term = dot(activated, hidden_grad, ((0,), (0,))) * grad_scale
    output_grad, middle_grad = lax.psum((output_term, middle_term), "seq")
    first_term = dot(activated, later, ((0,), (0,))) * grad_scale
    last_term = dot(activated, earlier, ((0,), (0,))) * grad_scale
    first_grad, last_grad = lax.psum((first_term, last_term), "seq")
    conv_grad = jnp.stack([first_grad, middle_grad, last_grad])

    input_gradient = (
        dot(hidden_grad, conv_weight[1], ((1,), (1,)))
        + dot(later, conv_weight[0], ((1,), (1,)))
        + dot(earlier, conv_weight[2], ((1,), (1,)))
    )
    weighted = input_gradient * gelu_slope(normed, normed_cdf) * norm_gain
    inner = jnp.mean(weighted * signal_f, axis=-1, keepdims=True)
    cubed = inverse_rms * inverse_rms * inverse_rms
    signal_grad = cotangent.astype(jnp.float32) + weighted * inverse_rms - signal_f * cubed * inner
    return (block_out, signal_grad.astype(jnp.bfloat16), conv_grad, output_grad)


def solution(mesh):
    placed = (P(("groups", "seq"), None), P(), P(), P(), P(("groups", "seq"), None))
    return jax.shard_map(
        shards,
        mesh=mesh,
        in_specs=placed,
        out_specs=(
            P(("groups", "seq"), None),
            P(("groups", "seq"), None),
            P("groups", None, None),
            P("groups", None),
        ),
        check_vma=False,
    )
```
